128 devices in a mesh: rows: 16 (over z, x), cols: 8 (over y, core).
Axes of the slice: x: 4, y: 4, z: 4, core: 2. Of those that a mesh axis runs over, the one named last changes fastest.
Arguments:
- points: float32 [160, 127], replicated, may hold values from -0.5 to 0.5
- noise: float32 [160, 128], replicated, may hold values from 0.3 to 3
- basis: float32 [20480, 128], P('rows'), may hold values from -0.5 to 0.5
Outputs:
- factor: float32 [20480, 20480], P('rows', 'cols')
The draws below stay inside these ranges and needn't reach their ends.
All inputs are finite; a program needn't handle non-finite values.
Results may differ from the reference program's by a relative error of at most 0.0003.
Values sent between devices are 32-bit elements; how exact they have to be, the bound alone decides.
A program may use at most 128 MiB of HBM per device.

```python
import math
import jax
import jax.numpy as jnp
from jax import lax

D = 127
W = 128
NB = 128
NPT = 160
PW = 256
PANELS = 2
ORDER = 20480
LEAD = 512


def shard_levels(key, shape, shards, smallest, high):
    gain, own = 1.0, jax.random.fold_in(key, 6)
    for axis_at, blocks in shards:
        draws = jnp.exp(jax.random.uniform(jax.random.fold_in(own, axis_at), (blocks,), jnp.float32, smallest / len(shards), high / len(shards)))
        gain = gain * jnp.repeat(draws, shape[axis_at] // blocks).reshape([-1 if axis == axis_at else 1 for axis in range(len(shape))])
    return gain


def gaussian(rng, shape, spread, bound, shards=(), kind=jnp.bfloat16):
    result = spread * jax.random.normal(rng, shape, jnp.float32)
    if shards:
        result = result * shard_levels(rng, shape, shards, -0.22, 0.18)
    return jnp.clip(result, -bound, bound).astype(kind)


def setup_inputs(seed: int = 0) -> dict:
    seeds = jax.random.split(jax.random.key(seed), 4)
    return {
        "points": gaussian(seeds[0], (NPT, D), D ** -0.5, 0.5, (), jnp.float32),
        "noise": jnp.clip(jnp.exp(jax.random.uniform(seeds[1], (NPT, W), jnp.float32, math.log(0.3), math.log(3.0))), 0.3, 3.0),
        "basis": gaussian(seeds[2], (ORDER, NB), NB ** -0.5, 0.5, ((0, 16),), jnp.float32),
    }


def tile_rows(point_row, col_points):
    rho = point_row[None, :] - col_points
    kval = jnp.exp(-0.5 * jnp.sum(rho * rho, axis=1))
    ones = jnp.ones((col_points.shape[0], 1), jnp.float32)
    left = jnp.concatenate([ones, -rho], axis=1)
    right = jnp.concatenate([ones, rho], axis=1)
    width = left.shape[1]
    jmat = jnp.diag((jnp.arange(width) > 0).astype(jnp.float32))
    tiles = kval[None, :, None] * (jmat[:, None, :] + left.T[:, :, None] * right[None, :, :])
    return tiles.reshape(width, -1)

def point_rows(point_row, noise_row, basis_row, start, col_points, col_basis, col_start):
    width = noise_row.shape[0]
    values = tile_rows(point_row, col_points) + jnp.dot(basis_row, col_basis.T, precision=lax.Precision.HIGHEST)
    row_ids = start + jnp.arange(width).astype(jnp.int32)
    col_ids = col_start + jnp.arange(values.shape[1]).astype(jnp.int32)
    same = row_ids[:, None] == col_ids[None, :]
    return values + jnp.where(same, noise_row[:, None], jnp.float32(0.0))

def assemble(points_rows, noise_rows, basis_rows, starts, col_points, col_basis, col_start):
    count, width = noise_rows.shape
    basis_split = basis_rows.reshape(count, width, -1)

    def single(items):
        return point_rows(items[0], items[1], items[2], items[3], col_points, col_basis, col_start)
    blocks = lax.map(single, (points_rows, noise_rows, basis_split, starts))
    return blocks.reshape(count * width, -1)

def factor_panels(columns, row_ids, panel_width, panels):
    lead = None
    for panel_index in range(panels):
        low = panel_index * panel_width
        block = columns[:, low:low + panel_width]
        if lead is not None:
            block = block - jnp.dot(lead, lead[low:low + panel_width].T, precision=lax.Precision.HIGHEST)
        diag = jnp.linalg.cholesky(block[low:low + panel_width])
        panel = lax.linalg.triangular_solve(diag, block, left_side=False, lower=True, transpose_a=True)
        col_ids = low + jnp.arange(panel_width).astype(jnp.int32)
        panel = jnp.where(row_ids[:, None] < col_ids[None, :], jnp.float32(0.0), panel)
        lead = panel if lead is None else jnp.concatenate([lead, panel], axis=1)
    return lead

def finish(points_rows, noise_rows, basis_rows, starts, lead_rows, col_points, col_basis, col_start, lead_cols):
    count, width = noise_rows.shape
    ncols = lead_cols.shape[0]
    leading = lead_rows.shape[1]
    cross = lead_cols.T
    col_ids = col_start + jnp.arange(ncols).astype(jnp.int32)

    def single(items):
        prow, nrow, brow, lrow, start = items
        values = point_rows(prow, nrow, brow, start, col_points, col_basis, col_start)
        trail = values - jnp.dot(lrow, cross, precision=lax.Precision.HIGHEST)
        row_ids = start + jnp.arange(width).astype(jnp.int32)
        own = jnp.pad(lrow, ((0, 0), (0, ncols - leading)))
        mirror = lax.dynamic_slice_in_dim(cross, jnp.minimum(start, leading - width).astype(jnp.int32), width, 0)
        inner = jnp.where(row_ids[:, None] < leading, mirror, trail)
        return jnp.where(col_ids[None, :] < leading, own, inner)
    blocks = lax.map(single, (points_rows, noise_rows, basis_rows.reshape(count, width, -1), lead_rows.reshape(count, width, leading), starts))
    return blocks.reshape(count * width, ncols)

def reference(points, noise, basis):
    count, width = noise.shape
    order = count * width
    lead_points = LEAD // width
    starts = (width * jnp.arange(count)).astype(jnp.int32)
    columns = assemble(points, noise, basis, starts, points[:lead_points], basis[:LEAD], 0)
    row_ids = jnp.arange(order).astype(jnp.int32)
    lead = factor_panels(columns, row_ids, PW, PANELS)
    return finish(points, noise, basis, starts, lead, points, basis, 0, lead)
```

```python
import functools

import jax
import jax.numpy as jnp
from jax import lax
from jax.experimental import pallas as pl
from jax.experimental.pallas import tpu as pltpu
from jax.sharding import PartitionSpec as P

W = 128
LEAD = 512
CHUNK = 256
HIGHEST = lax.Precision.HIGHEST
MESH = pl.DeviceIdType.MESH
F32 = jnp.float32
BF16 = jnp.bfloat16


def dot(a, b, dims=((1,), (0,))):
    return lax.dot_general(a, b, (dims, ((), ())), precision=HIGHEST, preferred_element_type=F32)


def eye_mask():
    return lax.broadcasted_iota(jnp.int32, (W, W), 0) == lax.broadcasted_iota(jnp.int32, (W, W), 1)


def row_terms(xr, xj, noise, same):
    lane = lax.broadcasted_iota(jnp.int32, xr.shape, 1)
    rho = xr - xj
    k = jnp.exp(-0.5 * jnp.sum(rho * rho, axis=1, keepdims=True))
    kq = k * jnp.where(lane == 0, 1.0, rho)
    diagonal = jnp.where(lane == 0, 0.0, jnp.broadcast_to(k, xr.shape))
    return kq, diagonal + jnp.where(same, noise, 0.0)


def tile(eye, p, kq, diagonal):
    return jnp.where(eye, diagonal, 0.0) + p * kq


def exchange_kernel(n, basis, top, cols, scatter_send, scatter_recv, own_sem, top_send, top_recv, col_send, col_recv):
    me = lax.axis_index("rows")
    col = lax.axis_index("cols")
    rows = basis.shape[0]
    tp = LEAD // n
    cp = rows // n

    barrier = pltpu.get_barrier_semaphore()
    for k in range(1, n):
        pl.semaphore_signal(barrier, inc=1, device_id={"rows": lax.rem(me + k, n)}, device_id_type=MESH)
    pl.semaphore_wait(barrier, n - 1)

    def top_piece(ref, d):
        return ref.at[pl.ds(pl.multiple_of(d * tp, tp), tp), :]

    def src_piece(d):
        return basis.at[pl.ds(pl.multiple_of(d * cp, cp), cp), :]

    def col_piece(t, d):
        return cols.at[pl.ds(pl.multiple_of(t * rows + d * cp, cp), cp), :]

    def remote(src, dst, ss, rs, dest):
        return pltpu.make_async_remote_copy(
            src_ref=src, dst_ref=dst, send_sem=ss, recv_sem=rs, device_id={"rows": dest}, device_id_type=MESH
        )

    @pl.when(me == 0)
    def _():
        for k in range(1, n):
            d = lax.rem(me + k, n)
            remote(top_piece(basis, d), top_piece(top, d), scatter_send.at[0, k], scatter_recv.at[0], d).start()
        pltpu.make_async_copy(top_piece(basis, me), top_piece(top, me), own_sem.at[0]).start()

    for t in range(2):

        @pl.when(me == 2 * col + t)
        def _():
            for k in range(1, n):
                d = lax.rem(me + k, n)
                remote(src_piece(d), col_piece(t, d), scatter_send.at[1 + t, k], scatter_recv.at[1 + t], d).start()
            pltpu.make_async_copy(src_piece(me), col_piece(t, me), own_sem.at[1 + t]).start()

    @pl.when(me != 0)
    def _():
        remote(top_piece(top, me), top_piece(top, me), scatter_send.at[0, 0], scatter_recv.at[0], me).wait_recv()

    @pl.when(me == 0)
    def _():
        pltpu.make_async_copy(top_piece(basis, me), top_piece(top, me), own_sem.at[0]).wait()

    for k in range(1, n):
        d = lax.rem(me + k, n)
        remote(top_piece(top, me), top_piece(top, me), top_send.at[k], top_recv.at[k], d).start()

    for t in range(2):

        @pl.when(me != 2 * col + t)
        def _():
            remote(col_piece(t, me), col_piece(t, me), scatter_send.at[1 + t, 0], scatter_recv.at[1 + t], me).wait_recv()

        @pl.when(me == 2 * col + t)
        def _():
            pltpu.make_async_copy(src_piece(me), col_piece(t, me), own_sem.at[1 + t]).wait()

    for t in range(2):
        for k in range(1, n):
            d = lax.rem(me + k, n)
            remote(col_piece(t, me), col_piece(t, me), col_send.at[t, k], col_recv.at[t, k], d).start()

    for k in range(1, n):
        s = lax.rem(me + n - k, n)
        remote(top_piece(top, s), top_piece(top, s), top_send.at[k], top_recv.at[k], s).wait_recv()
    for t in range(2):
        for k in range(1, n):
            s = lax.rem(me + n - k, n)
            remote(col_piece(t, s), col_piece(t, s), col_send.at[t, k], col_recv.at[t, k], s).wait_recv()
    for k in range(1, n):
        remote(top_piece(top, me), top_piece(top, me), top_send.at[k], top_recv.at[k], me).wait_send()
    for t in range(2):
        for k in range(1, n):
            remote(col_piece(t, me), col_piece(t, me), col_send.at[t, k], col_recv.at[t, k], me).wait_send()

    @pl.when(me == 0)
    def _():
        for k in range(1, n):
            d = lax.rem(me + k, n)
            remote(top_piece(basis, d), top_piece(top, d), scatter_send.at[0, k], scatter_recv.at[0], d).wait_send()

    for t in range(2):

        @pl.when(me == 2 * col + t)
        def _():
            for k in range(1, n):
                d = lax.rem(me + k, n)
                remote(src_piece(d), col_piece(t, d), scatter_send.at[1 + t, k], scatter_recv.at[1 + t], d).wait_send()


def exchange(basis, n):
    vmem = pl.BlockSpec(memory_space=pltpu.VMEM)
    dma = pltpu.SemaphoreType.DMA
    return pl.pallas_call(
        functools.partial(exchange_kernel, n),
        out_shape=(
            jax.ShapeDtypeStruct((LEAD, W), F32),
            jax.ShapeDtypeStruct((2 * basis.shape[0], W), F32),
        ),
        in_specs=[vmem],
        out_specs=(vmem, vmem),
        scratch_shapes=[dma((3, n)), dma((3,)), dma((3,)), dma((n,)), dma((n,)), dma((2, n)), dma((2, n))],
        compiler_params=pltpu.CompilerParams(collective_id=0, has_side_effects=True),
        name="exchange",
    )(basis)


def factor_block(d):
    nb = W // 8
    a = [d[8 * i : 8 * i + 8, :] for i in range(nb)]
    lane = lax.broadcasted_iota(jnp.int32, (8, W), 1)
    sub = lax.broadcasted_iota(jnp.int32, (8, W), 0)
    e = [jnp.where(lane == sub + 8 * i, 1.0, 0.0).astype(F32) for i in range(nb)]
    scales = []
    for k in range(W):
        b, o = divmod(k, 8)
        col = [jnp.broadcast_to(a[i][:, k : k + 1], (8, W)) for i in range(b, nb)]
        pivot = jnp.broadcast_to(col[0][o : o + 1, :], (8, W))
        inv = 1.0 / pivot
        scales.append(lax.rsqrt(pivot[0:1, :]))
        arow = jnp.broadcast_to(a[b][o : o + 1, :], (8, W)) * inv
        erow = jnp.broadcast_to(e[b][o : o + 1, :], (8, W)) * inv
        for i in range(b, nb):
            c = col[i - b]
            if i == b:
                c = jnp.where(sub > o, c, 0.0)
            a[i] = a[i] - c * arow
            e[i] = e[i] - c * erow
    scale = [jnp.concatenate(scales[8 * i : 8 * i + 8], axis=0) for i in range(nb)]
    return jnp.concatenate([e[i] * scale[i] for i in range(nb)], axis=0)


def factor_kernel(top, xlead, xb, noise, out, s):
    eye = eye_mask()
    first = lax.broadcasted_iota(jnp.int32, (W, W), 0) == 0
    nlead = LEAD // W
    s[:, :LEAD] = dot(top[...], top[...], ((1,), (1,)))
    point = lax.broadcasted_iota(jnp.int32, (8, 1), 0)
    for j in range(nlead):
        kq, diagonal = row_terms(xlead[...], xlead[j : j + 1, :], noise[...], point == j)
        pj = jnp.where(first, 1.0, xb[j * W : (j + 1) * W, :])
        for i in range(nlead):
            p = pj - xb[i * W : (i + 1) * W, :]
            s[i * W : (i + 1) * W, j * W : (j + 1) * W] += tile(eye, p, kq[i : i + 1, :], diagonal[i : i + 1, :])
    ids = lax.broadcasted_iota(jnp.int32, (LEAD, LEAD), 0) == lax.broadcasted_iota(jnp.int32, (LEAD, LEAD), 1)
    s[:, LEAD:] = jnp.where(ids, 1.0, 0.0).astype(F32)
    lanes = lax.broadcasted_iota(jnp.int32, (W, LEAD), 1)

    def step(kb, _):
        at = pl.multiple_of(kb * W, W)
        inverse = factor_block(s[pl.ds(at, W), pl.ds(at, W)])
        panel = dot(inverse, s[pl.ds(at, W), :])
        coef = jnp.where(lanes >= (kb + 1) * W, panel[:, :LEAD], 0.0)
        s[...] -= dot(coef, panel, ((0,), (0,)))
        s[pl.ds(at, W), :] = panel
        return 0

    lax.fori_loop(0, nlead, step, 0)
    out[...] = s[:, LEAD:]


def factor(top, xlead, xb, noise):
    vmem = pl.BlockSpec(memory_space=pltpu.VMEM)
    return pl.pallas_call(
        factor_kernel,
        out_shape=jax.ShapeDtypeStruct((LEAD, LEAD), F32),
        in_specs=[vmem] * 4,
        out_specs=vmem,
        scratch_shapes=[pltpu.VMEM((LEAD, 2 * LEAD), F32)],
        compiler_params=pltpu.CompilerParams(vmem_limit_bytes=32 << 20),
        name="factor",
    )(top, xlead, xb, noise)


def split(v):
    hi = v.astype(BF16)
    return hi, (v - hi.astype(F32)).astype(BF16)


def main_kernel(row_pts, basis, top, inv, colb, xrow, xcol, xlead, xbrow, xbcol, xblead, noise_row, noise_lead, out, lead, lhs, rhs):
    row_pos = lax.axis_index("rows")
    col_pos = lax.axis_index("cols")
    step = pl.program_id(0)
    eye = eye_mask()
    first = lax.broadcasted_iota(jnp.int32, (W, W), 0) == 0
    nlead = LEAD // W
    half = LEAD // 2
    width = W + LEAD
    rpoint = row_pos * row_pts + lax.broadcasted_iota(jnp.int32, (xrow.shape[0], 1), 0)
    lpoint = lax.broadcasted_iota(jnp.int32, (xlead.shape[0], 1), 0)

    @pl.when(step == 0)
    def _():
        lead[...] = dot(basis[...], top[...], ((1,), (1,)))
        for j in range(nlead):
            kq, diagonal = row_terms(xrow[...], xlead[j : j + 1, :], noise_row[...], rpoint == j)
            pj = jnp.where(first, 1.0, xblead[j * W : (j + 1) * W, :])
            for i in range(row_pts):
                p = pj - xbrow[i * W : (i + 1) * W, :]
                lead[i * W : (i + 1) * W, j * W : (j + 1) * W] += tile(eye, p, kq[i : i + 1, :], diagonal[i : i + 1, :])

        def rows(i, _):
            at = pl.ds(pl.multiple_of(i * CHUNK, CHUNK), CHUNK)
            a = lead[at, :]
            left = dot(a[:, :half], inv[:half, :half], ((1,), (1,)))
            right = dot(a, inv[half:, :], ((1,), (1,)))
            lead[at, :half] = left
            lead[at, half:] = right
            for v, o in ((basis[at, :], 0), (left, W), (right, W + half)):
                hi, lo = split(v)
                n = v.shape[1]
                lhs[at, o : o + n] = hi
                lhs[at, width + o : width + o + n] = lo
                lhs[at, 2 * width + o : 2 * width + o + n] = hi
            return 0

        lax.fori_loop(0, basis.shape[0] // CHUNK, rows, 0)

    is_lead = jnp.logical_and(col_pos == 0, step < LEAD // CHUNK)

    @pl.when(is_lead)
    def _():
        cols = lax.broadcasted_iota(jnp.int32, (CHUNK, CHUNK), 1) + step * CHUNK
        at = pl.ds(pl.multiple_of(step * CHUNK, CHUNK), CHUNK)
        for i in range(basis.shape[0] // CHUNK):
            ids = lax.broadcasted_iota(jnp.int32, (CHUNK, CHUNK), 0) + i * CHUNK + row_pos * basis.shape[0]
            out[i * CHUNK : (i + 1) * CHUNK, :] = jnp.where(ids < cols, 0.0, lead[i * CHUNK : (i + 1) * CHUNK, at])

    @pl.when(jnp.logical_not(is_lead))
    def _():
        cb = colb[...]
        across = dot(top[...], cb, ((1,), (1,)))
        per = CHUNK // W
        base = step * per
        points = [xcol[pl.ds(base + t, 1), :] for t in range(per)]
        pjs = [jnp.where(first, 1.0, xbcol[t * W : (t + 1) * W, :]) for t in range(per)]
        ids = [col_pos * (row_pts * 2) + base + t for t in range(per)]
        terms = [row_terms(xlead[...], points[t], noise_lead[...], lpoint == ids[t]) for t in range(per)]
        pieces = []
        for i in range(nlead):
            strip = []
            for t in range(per):
                p = pjs[t] - xblead[i * W : (i + 1) * W, :]
                strip.append(tile(eye, p, terms[t][0][i : i + 1, :], terms[t][1][i : i + 1, :]))
            pieces.append(jnp.concatenate(strip, axis=1))
        across = across + jnp.concatenate(pieces, axis=0)
        upper = dot(inv[:half, :half], across[:half, :])
        lower = dot(inv[half:, :], across)
        hi, lo = split(cb.T)
        rhs[0:W, :] = hi
        rhs[width : width + W, :] = hi
        rhs[2 * width : 2 * width + W, :] = lo
        for v, o in ((upper, W), (lower, W + half)):
            hi, lo = split(-v)
            rhs[o : o + half, :] = hi
            rhs[width + o : width + o + half, :] = hi
            rhs[2 * width + o : 2 * width + o + half, :] = lo
        terms = [row_terms(xrow[...], points[t], noise_row[...], rpoint == ids[t]) for t in range(per)]
        two = CHUNK // W
        for i in range(row_pts // two):
            at = slice(i * CHUNK, (i + 1) * CHUNK)
            total = jnp.dot(lhs[at, :], rhs[...], preferred_element_type=F32)
            for u in range(two):
                q = i * two + u
                for t in range(per):
                    p = pjs[t] - xbrow[q * W : (q + 1) * W, :]
                    v = tile(eye, p, terms[t][0][q : q + 1, :], terms[t][1][q : q + 1, :])
                    out[q * W : (q + 1) * W, t * W : (t + 1) * W] = total[u * W : (u + 1) * W, t * W : (t + 1) * W] + v

        @pl.when(row_pos == 0)
        def _():
            out[:half, :] = upper
            out[half:LEAD, :] = lower


def main(row_pts, basis, top, inv, colb, xrow, xcol, xlead, xbrow, xbcol, xblead, noise_row, noise_lead):
    rows, cols = basis.shape[0], colb.shape[0]
    width = W + LEAD

    def whole(v):
        return pl.BlockSpec(v.shape, lambda j: (0, 0), pipeline_mode=pl.Buffered(1))

    chunk = pl.BlockSpec((CHUNK, W), lambda j: (j, 0))
    return pl.pallas_call(
        functools.partial(main_kernel, row_pts),
        out_shape=jax.ShapeDtypeStruct((rows, cols), F32),
        grid=(cols // CHUNK,),
        in_specs=[whole(basis), whole(top), whole(inv), chunk, whole(xrow), whole(xcol), whole(xlead), whole(xbrow), chunk, whole(xblead), whole(noise_row), whole(noise_lead)],
        out_specs=pl.BlockSpec((rows, CHUNK), lambda j: (0, j)),
        scratch_shapes=[
            pltpu.VMEM((rows, LEAD), F32),
            pltpu.VMEM((rows, 3 * width), BF16),
            pltpu.VMEM((3 * width, CHUNK), BF16),
        ],
        compiler_params=pltpu.CompilerParams(vmem_limit_bytes=48 << 20),
        name="output",
    )(basis, top, inv, colb, xrow, xcol, xlead, xbrow, xbcol, xblead, noise_row, noise_lead)


def pad_rows(v, n):
    return jnp.pad(v, ((0, n - v.shape[0]), (0, 0)))


def body(points, noise, basis):
    row_pos = lax.axis_index("rows")
    col_pos = lax.axis_index("cols")
    n = lax.axis_size("rows")
    row_pts = basis.shape[0] // W
    col_pts = 2 * row_pts
    nlead = LEAD // W
    x = jnp.pad(points, ((0, 0), (1, 0)))
    xrow = lax.dynamic_slice_in_dim(x, row_pos * row_pts, row_pts, 0)
    xcol = lax.dynamic_slice_in_dim(x, col_pos * col_pts, col_pts, 0)
    nrow = lax.dynamic_slice_in_dim(noise, row_pos * row_pts, row_pts, 0)

    def spread(v):
        return jnp.broadcast_to(v[:, :, None], v.shape + (W,)).reshape(-1, W)

    xlead = x[:nlead]
    xblead = spread(xlead)
    top, cols = exchange(basis, n)
    inv = factor(top, pad_rows(xlead, 8), xblead, pad_rows(noise[:nlead], 8))
    return main(
        row_pts, basis, top, inv, cols, pad_rows(xrow, 16), pad_rows(xcol, 24), pad_rows(xlead, 8),
        spread(xrow), spread(xcol), xblead, pad_rows(nrow, 16), pad_rows(noise[:nlead], 8),
    )


def solution(mesh):
    placed = (P(), P(), P("rows", None))
    return jax.shard_map(body, mesh=mesh, in_specs=placed, out_specs=P("rows", "cols"), check_vma=False)
```
